768 devices in a mesh: dp: 16 (over z_lo, x), fsdp: 48 (over y, z_hi, core).
Axes of the slice: x: 4, y: 8, z: 12 (z_hi: 3, z_lo: 4; z = z_hi * 4 + z_lo), core: 2. Of those that a mesh axis runs over, the one named last changes fastest.
Arguments:
- hidden: bfloat16 [768, 256, 5120], P(('dp', 'fsdp')), may hold values from -6 to 6
- queries: bfloat16 [768, 256, 1024], P(('dp', 'fsdp')), may hold values from -6 to 6
- upstream: bfloat16 [768, 256, 1024], P(('dp', 'fsdp')), may hold values from -0.3984375 to 0.3984375
- advantage: float32 [768, 256], P(('dp', 'fsdp')), may hold values from -5 to 5
- selected: int32 [768, 256], P(('dp', 'fsdp')), may hold values from 0 to 1, as said below
- segment: int32 [768, 256], P(('dp', 'fsdp')), may hold values from 0 to 3, never falling along the last dimension, each value on 1 to 128 neighbouring positions
- w_kv: bfloat16 [5376, 256], P('fsdp'), may hold values from -0.078125 to 0.078125
- k_gain: float32 [128], replicated, may hold values from 0.25 to 1.75
- q_gain: float32 [128], replicated, may hold values from 0.25 to 1.75
Outputs:
- d_weight: float32 [5376, 256], P('fsdp')
- d_gain: float32 [128], replicated
The draws below stay inside these ranges and needn't reach their ends.
Inputs may be any that keep to these rules, and one draw needn't show every extreme that they name: Each row has at most 128 selected tokens, and some row has exactly 128.
All inputs are finite; a program needn't handle non-finite values.
Results may differ from the reference program's by a relative error of at most 0.007.
Values may be sent and summed in bfloat16 or wider, within the bound.
No kernel may reach another device: no remote copies, remote signals or barrier semaphores. Data moves between devices by JAX's collectives and lax.ppermute only.
A program may use at most 32 MiB of HBM per device.

```python
import math
import jax
import jax.numpy as jnp
import numpy as np
from jax import lax

D = 5120
GROUP = 8
HD = 128
TOK_DEV = 256
SEGS = 4
CAP = 128
ROWS = 768
D_PAD = 5376


def draw_selected(key, part):
    key_count = jax.random.fold_in(key, 101)
    key_top = jax.random.fold_in(key, 202)
    key_order = jax.random.fold_in(key, 303)
    spread = jax.random.randint(key_count, (ROWS,), 0, CAP)
    counts = 1 + spread * (spread + CAP) // (2 * CAP)
    busiest = jax.random.randint(key_top, (), 0, ROWS)
    counts = jnp.where(jnp.arange(ROWS) == busiest, CAP, counts)
    row_keys = jax.random.split(key_order, ROWS)
    orders = jax.vmap(lambda one_key: jax.random.permutation(one_key, TOK_DEV))(row_keys)
    ranks = jnp.argsort(orders, axis=1, stable=True)
    return (ranks < counts[:, None]).astype(jnp.int32)


def block_scale(key, extent, pieces, smallest, largest):
    gain, own = 1.0, jax.random.fold_in(key, 6)
    for position, parts in pieces:
        steps = jnp.exp(jax.random.uniform(jax.random.fold_in(own, position), (parts,), jnp.float32, smallest / len(pieces), largest / len(pieces)))
        gain = gain * jnp.repeat(steps, extent[position] // parts).reshape([-1 if axis == position else 1 for axis in range(len(extent))])
    return gain


def length_profile(count, total, limit, skew):
    portions = [(1 << 20) // math.isqrt(rank ** skew) + 1 for rank in range(2, count + 1)]
    spare, given = total - limit - (count - 1), [1] * (count - 1)
    while spare > 0:
        movable = [i for i in range(count - 1) if given[i] < limit]
        pool, remaining = sum([portions[i] for i in movable]), spare
        for i in movable:
            addition = min(limit - given[i], max(1, remaining * portions[i] // pool), spare)
            given[i] = given[i] + addition
            spare = spare - addition
    return np.array([limit] + given)


def ragged(rng, count, total, bound, slope):
    if count == 2:
        one = jax.random.randint(rng, (), max(1, total - bound), min(bound, total - 1) + 1)
        return jnp.stack([one, total - one])
    tallies = jnp.asarray(length_profile(count, total, bound, slope), jnp.int32)
    twos = (count - 1) // 2
    giver, receiver = tallies[1:1 + 2 * twos:2], tallies[2:2 + 2 * twos:2]
    room = jnp.minimum(giver - 1, bound - receiver)
    shifted = jax.random.randint(jax.random.fold_in(rng, 1), (twos,), 0, 1 << 20) % (room + 1)
    tallies = tallies.at[1:1 + 2 * twos:2].set(giver - shifted).at[2:2 + 2 * twos:2].set(receiver + shifted)
    return tallies[jax.random.permutation(jax.random.fold_in(rng, 2), count)]


def noise(stream_key, extent, width, bound, cuts=(), held_as=jnp.bfloat16):
    array = jax.random.normal(stream_key, extent, jnp.float32) * width
    if len(cuts) > 0:
        array = block_scale(stream_key, extent, cuts, -0.22, 0.18) * array
    return jnp.clip(array, min=-bound, max=bound).astype(held_as)


def setup_inputs(seed: int = 0) -> dict:
    streams_of = jax.random.split(jax.random.key(seed), 10)
    hidden = noise(streams_of[0], (ROWS, TOK_DEV, D), 1.0, 6.0, ((0, 768),))
    queries = noise(streams_of[1], (ROWS, TOK_DEV, GROUP * HD), 1.0, 6.0, ((0, 768),))
    upstream = noise(streams_of[2], (ROWS, TOK_DEV, GROUP * HD), 0.05, 0.3984375, ((0, 768),))
    advantage = noise(streams_of[3], (ROWS, TOK_DEV), 1.0, 5.0, ((0, 768),), jnp.float32)
    selected = draw_selected(jax.random.fold_in(streams_of[9], 71), 0)
    segment = jax.vmap(lambda own: jnp.searchsorted(jnp.cumsum(ragged(own, SEGS, TOK_DEV, TOK_DEV // 2, 1)), jnp.arange(TOK_DEV), side="right"))(jax.random.split(streams_of[5], ROWS)).reshape((ROWS, TOK_DEV)).astype(jnp.int32)
    w_kv = noise(streams_of[6], (D_PAD, 2 * HD), D ** -0.5, 0.078125, ((0, 48),))
    k_gain = jnp.clip(1.0 + 0.15 * jax.random.normal(streams_of[7], (HD,), jnp.float32), 0.25, 1.75)
    q_gain = jnp.clip(1.0 + 0.15 * jax.random.normal(streams_of[8], (HD,), jnp.float32), 0.25, 1.75)
    return dict(hidden=hidden, queries=queries, upstream=upstream, advantage=advantage, selected=selected, segment=segment, w_kv=w_kv, k_gain=k_gain, q_gain=q_gain)


epsilon = 1e-06

def reference(hidden, queries, upstream, advantage, selected, segment, w_kv, k_gain, q_gain):
    weight = w_kv[:D]
    score_scale = HD ** (-0.5)

    def one_row(carry, inputs):
        total_w, total_g = carry
        hidden_row, query_row, upstream_row, advantage_row, selected_row, segment_row = inputs
        key_value = jnp.dot(hidden_row, weight, preferred_element_type=jnp.float32)
        k_raw = key_value[:, :HD]
        k_scale = lax.rsqrt(lax.optimization_barrier(jnp.mean(k_raw * k_raw, axis=-1, keepdims=True)) + epsilon)
        k_hat = k_raw * k_scale
        k_norm = (k_hat * k_gain).astype(jnp.bfloat16)
        values = key_value[:, HD:].astype(jnp.bfloat16)
        query_full = query_row.reshape(TOK_DEV, GROUP, HD).astype(jnp.float32)
        q_scale = lax.rsqrt(lax.optimization_barrier(jnp.mean(query_full * query_full, axis=-1, keepdims=True)) + epsilon)
        q_norm = (query_full * q_scale * q_gain).astype(jnp.bfloat16)
        token_weight = advantage_row * selected_row.astype(jnp.float32)
        cotangent = (token_weight[:, None] * upstream_row.astype(jnp.float32)).astype(jnp.bfloat16)
        cotangent = cotangent.reshape(TOK_DEV, GROUP, HD)
        positions = jnp.arange(TOK_DEV, dtype=jnp.int32)
        allowed = (segment_row[:, None] == segment_row[None, :]) & (positions[None, :] <= positions[:, None])
        scores = jnp.einsum('qhd,kd->hqk', q_norm.astype(jnp.float32), k_norm.astype(jnp.float32)) * score_scale
        expo = jnp.where(allowed[None], jnp.exp(scores), 0.0)
        probs = expo / lax.optimization_barrier(jnp.sum(expo, axis=-1, keepdims=True))
        probs_b = probs.astype(jnp.bfloat16)
        outputs = jnp.einsum('hqk,kd->qhd', probs_b.astype(jnp.float32), values.astype(jnp.float32))
        delta = lax.optimization_barrier(jnp.sum(cotangent.astype(jnp.float32) * outputs, axis=-1))
        dprob = jnp.einsum('qhd,kd->hqk', cotangent.astype(jnp.float32), values.astype(jnp.float32))
        dscore = (probs * (dprob - delta.T[:, :, None]) * score_scale).astype(jnp.bfloat16)
        d_key = jnp.einsum('hqk,qhd->kd', dscore.astype(jnp.float32), q_norm.astype(jnp.float32))
        d_value = jnp.einsum('hqk,qhd->kd', probs_b.astype(jnp.float32), cotangent.astype(jnp.float32))
        d_khat = d_key * k_gain
        gain_term = lax.optimization_barrier(jnp.sum(d_key * k_hat, axis=0))
        d_kraw = k_scale * (d_khat - k_hat * lax.optimization_barrier(jnp.mean(d_khat * k_hat, axis=-1, keepdims=True)))
        d_kv = jnp.concatenate([d_kraw, d_value], axis=1).astype(jnp.bfloat16)
        total_w = total_w + jnp.dot(hidden_row.T, d_kv, preferred_element_type=jnp.float32)
        return ((total_w, total_g + gain_term), None)
    start = (jnp.zeros((D, 2 * HD), jnp.float32), jnp.zeros((HD,), jnp.float32))
    (total_w, total_g), _ = lax.scan(one_row, start, (hidden, queries, upstream, advantage, selected, segment))
    d_weight = jnp.concatenate([total_w, jnp.zeros((D_PAD - D, 2 * HD), jnp.float32)], axis=0)
    return (d_weight, total_g)
```

```python
import jax
import jax.numpy as jnp
from jax import lax
from jax.experimental import pallas as pl
from jax.experimental.pallas import tpu as pltpu
from jax.sharding import Mesh, PartitionSpec as P

EPS = 1e-06
HD = 128
GROUP = 8
TOK = 256
D = 5120
OWN = 112
HALF = OWN // 2
NEAR = 8
FAR = 12
BODY = FAR * HALF
SPAN = 48 * OWN
AXES = ("zh", "zl", "xh", "xl", "yh", "yl", "zhi", "core")
PAIRS = ("zl", "xl", "yl")

f32 = jnp.float32
bf16 = jnp.bfloat16
vmem = pl.BlockSpec(memory_space=pltpu.VMEM)
smem = pl.BlockSpec(memory_space=pltpu.SMEM)


def dot(a, b, ca, cb):
    return lax.dot_general(a, b, (((ca,), (cb,)), ((), ())), preferred_element_type=f32)


def column(row):
    return jnp.transpose(jnp.broadcast_to(row, (HD, TOK)))


def first_row(far, yl):
    return ((far // 3) * 6 + yl * 3 + far % 3) * (2 * OWN)


def place(w, ref, parity):
    def step(far, _):
        for yl in range(2):
            base = first_row(far, yl)
            row = pl.multiple_of(base + parity * OWN, 16)
            for ch in range(2):
                both = jnp.concatenate([ref[4 * ch + yl, far].astype(f32), ref[4 * ch + 2 + yl, far].astype(f32)], axis=0)
                w[pl.ds(row, OWN), ch * HD : (ch + 1) * HD] = both.astype(bf16)
            gap = pl.multiple_of(base + (1 - parity) * OWN, 16)
            w[pl.ds(gap, OWN), :] = jnp.zeros((OWN, 2 * HD), bf16)
        return 0

    lax.fori_loop(0, FAR, step, 0)


def prepare_body(where_ref, hidden, queries, upstream, advantage, selected, q_gain, own, q_out, cot_out, kv_out, w):
    place(w, own, where_ref[0])
    kv_out[...] = dot(hidden[...], w[:D, :], 1, 0)
    weight = column(advantage[...] * selected[...].astype(f32))
    for h in range(GROUP):
        cols = slice(h * HD, (h + 1) * HD)
        query = queries[:, cols].astype(f32)
        q_scale = lax.rsqrt(jnp.mean(query * query, axis=-1, keepdims=True) + EPS)
        q_out[:, cols] = (query * q_scale * q_gain[...]).astype(bf16)
        cot_out[:, cols] = (weight * upstream[:, cols].astype(f32)).astype(bf16)


def backward_body(where_ref, hidden, q_norms, cots, kv_part, segment, k_gain, other, keep, send, w, acc):
    core = where_ref[0]
    place(w, other, 1 - core)
    kv = kv_part[...] + dot(hidden[...], w[:D, :], 1, 0)
    k_raw = kv[:, :HD]
    k_scale = lax.rsqrt(jnp.mean(k_raw * k_raw, axis=-1, keepdims=True) + EPS)
    k_hat = k_raw * k_scale
    k_norm = (k_hat * k_gain[...]).astype(bf16)
    values = kv[:, HD:].astype(bf16)
    seg = segment[...].astype(f32)
    seg_col = column(seg)
    s_col = lax.broadcasted_iota(jnp.int32, (TOK, HD), 0)
    t_row = lax.broadcasted_iota(jnp.int32, (TOK, HD), 1)
    allowed = jnp.concatenate(
        [(seg_col == seg[:, i * HD : (i + 1) * HD]) & (s_col <= t_row + i * HD) for i in range(2)], axis=1
    )
    scale = HD ** (-0.5)
    d_key = jnp.zeros((TOK, HD), f32)
    d_value = jnp.zeros((TOK, HD), f32)
    for h in range(GROUP):
        cols = slice(h * HD, (h + 1) * HD)
        q_norm = q_norms[:, cols]
        cot = cots[:, cols]
        expo = jnp.where(allowed, jnp.exp(dot(k_norm, q_norm, 1, 1) * scale), 0.0)
        probs = expo * (1.0 / jnp.sum(expo, axis=0, keepdims=True))
        probs_b = probs.astype(bf16)
        dprob = dot(values, cot, 1, 1)
        delta = jnp.sum(probs_b.astype(f32) * dprob, axis=0, keepdims=True)
        dscore = (probs * (dprob - delta) * scale).astype(bf16)
        d_key = d_key + dot(dscore, q_norm, 1, 0)
        d_value = d_value + dot(probs_b, cot, 1, 0)
    gain = jnp.sum(d_key * k_hat, axis=0, keepdims=True)
    d_khat = d_key * k_gain[...]
    d_kraw = k_scale * (d_khat - k_hat * jnp.mean(d_khat * k_hat, axis=-1, keepdims=True))
    d_kv = jnp.concatenate([d_kraw, d_value], axis=1).astype(bf16)
    chunk = 1024
    for j in range(D // chunk):
        acc[j * chunk : (j + 1) * chunk, :] = dot(hidden[:, j * chunk : (j + 1) * chunk], d_kv, 0, 0)
    acc[D:SPAN, :] = jnp.zeros((SPAN - D, 2 * HD), f32)

    def put(far, _):
        for yl in range(2):
            base = first_row(far, yl)
            for parity, ref in ((core, keep), (1 - core, send)):
                for q in range(4):
                    row = pl.multiple_of(base + parity * OWN + (q % 2) * HALF, 8)
                    ref[2 * q + yl, far] = acc[pl.ds(row, HALF), (q // 2) * HD : (q // 2 + 1) * HD].astype(bf16)
        return 0

    lax.fori_loop(0, FAR, put, 0)
    high = gain.astype(bf16).astype(f32)
    line = lax.broadcasted_iota(jnp.int32, (HALF, HD), 0)
    rows = jnp.where(line == 0, high, jnp.where(line == 1, gain - high, 0.0)).astype(bf16)
    keep[1, FAR - 1] = rows
    send[1, FAR - 1] = rows


def gain_rows(pair):
    total = pair[0:1] + pair[1:2]
    high = total.astype(bf16).astype(f32)
    line = lax.broadcasted_iota(jnp.int32, (8, HD), 0)
    return jnp.where(line == 0, high, jnp.where(line == 1, total - high, 0.0))


def near_body(keep, received, blocks):
    tail = gain_rows(keep[1, FAR - 1, 0:8].astype(f32) + received[1, FAR - 1, 0:8].astype(f32))
    for i in range(NEAR):
        total = (keep[i].astype(f32) + received[i].astype(f32)).reshape(BODY, HD)
        blocks[i] = jnp.concatenate([total, tail], axis=0).astype(bf16)


def far_body(where_ref, received, blocks):
    tail = gain_rows(sum(received[i, BODY : BODY + 8].astype(f32) for i in range(NEAR)))
    for far in range(FAR):
        total = sum(received[i, far * HALF : (far + 1) * HALF].astype(f32) for i in range(NEAR))
        if far == FAR - 1:
            total = jnp.where(where_ref[1] == 1, 0.0, total)
        blocks[far] = jnp.concatenate([total, tail], axis=0).astype(bf16)


def last_body(received, blocks):
    total = sum(received[i].astype(f32) for i in range(FAR))
    whole = jnp.concatenate([total[:HALF], gain_rows(total[HALF:])], axis=0).astype(bf16)
    for i in range(16):
        blocks[i] = whole


def finish_body(spread, d_weight, d_gain):
    total = [sum(spread[8 * (i // 2) + 4 * (q // 2) + 2 * (i % 2) + q % 2].astype(f32) for i in range(4)) for q in range(4)]
    for q in range(4):
        row, col = (q % 2) * HALF, (q // 2) * HD
        d_weight[row : row + HALF, col : col + HD] = total[q][:HALF]
    d_gain[...] = total[0][HALF : HALF + 1] + total[0][HALF + 1 : HALF + 2]


def call(body, out, n_vector, scratch, limit, name, scalars=0):
    return pl.pallas_call(
        body,
        out_shape=out,
        in_specs=[smem] * scalars + [vmem] * n_vector,
        out_specs=jax.tree.map(lambda _: vmem, out),
        scratch_shapes=scratch,
        compiler_params=pltpu.CompilerParams(vmem_limit_bytes=limit << 20),
        name=name,
    )


def shape(*dims, dtype=bf16):
    return jax.ShapeDtypeStruct(dims, dtype)


def exchange(x, axes):
    return lax.all_to_all(x, axes, 0, 0, tiled=True)


def swap(x):
    return lax.ppermute(x, "core", [(0, 1), (1, 0)])


def shards(hidden, queries, upstream, advantage, selected, segment, w_kv, k_gain, q_gain):
    where = jnp.stack([lax.axis_index("core"), lax.axis_index("yl")]).astype(jnp.int32)
    mine = lax.dynamic_slice(w_kv, (lax.axis_index("xl") * HALF, lax.axis_index("zl") * HD), (HALF, HD))
    part = exchange(jnp.broadcast_to(mine[None], (FAR, HALF, HD)), ("yh", "zhi"))
    own = exchange(jnp.broadcast_to(part[None], (NEAR, FAR, HALF, HD)), PAIRS)
    other = swap(own)
    w_scratch = pltpu.VMEM((SPAN, 2 * HD), bf16)
    q_norms, cots, kv_part = call(
        prepare_body, (shape(TOK, GROUP * HD), shape(TOK, GROUP * HD), shape(TOK, 2 * HD, dtype=f32)), 7, [w_scratch], 16, "prepare", 1
    )(where, hidden[0], queries[0], upstream[0], advantage, selected, q_gain[None], own)
    piece = shape(NEAR, FAR, HALF, HD)
    keep, send = call(backward_body, (piece, piece), 7, [w_scratch, pltpu.VMEM((SPAN, 2 * HD), f32)], 24, "backward", 1)(
        where, hidden[0], q_norms, cots, kv_part, segment, k_gain[None], other
    )
    blocks = call(near_body, shape(NEAR, BODY + 8, HD), 2, [], 12, "near")(keep, swap(send))
    blocks = call(far_body, shape(FAR, HALF + 8, HD), 1, [], 12, "far", 1)(where, exchange(blocks, PAIRS))
    blocks = call(last_body, shape(16, HALF + 8, HD), 1, [], 8, "last")(exchange(blocks, ("yh", "zhi")))
    spread = exchange(blocks, ("zh", "zl", "xh", "xl"))
    d_weight, d_gain = call(finish_body, (shape(OWN, 2 * HD, dtype=f32), shape(1, HD, dtype=f32)), 1, [], 4, "finish")(spread)
    return (d_weight, d_gain[0])


def solution(mesh):
    fine = Mesh(mesh.devices.reshape(2, 2, 2, 2, 4, 2, 3, 2), AXES)
    rows = P(AXES, None, None)
    flat = P(AXES, None)
    owners = P(("yh", "yl", "zhi", "core"), None)
    in_specs = (rows, rows, rows, flat, flat, flat, owners, P(), P())
    return jax.shard_map(shards, mesh=fine, in_specs=in_specs, out_specs=(owners, P()), check_vma=False)
```

```python
import jax
import jax.numpy as jnp
import numpy as np
from jax import lax
from jax.experimental import pallas as pl
from jax.experimental.pallas import tpu as pltpu
from jax.sharding import Mesh, PartitionSpec as P

EPS = 1e-06
HD = 128
GROUP = 8
TOK = 256
D = 5120
OWN = 112
HALF = OWN // 2
NEAR = 8
FAR = 12
BODY = FAR * HALF
SPAN = 48 * OWN
AXES = ("zh", "zl", "xh", "xl", "yh", "yl", "zhi", "core")

f32 = jnp.float32
bf16 = jnp.bfloat16
vmem = pl.BlockSpec(memory_space=pltpu.VMEM)


def dot(a, b, ca, cb):
    return lax.dot_general(a, b, (((ca,), (cb,)), ((), ())), preferred_element_type=f32)


def column(row):
    return jnp.transpose(jnp.broadcast_to(row, (HD, TOK)))


def first_row(far, yl):
    return ((far // 3) * 6 + yl * 3 + far % 3) * (2 * OWN)


def place(w, ref, parity):
    def step(far, _):
        for yl in range(2):
            base = first_row(far, yl)
            row = pl.multiple_of(base + parity * OWN, 16)
            for ch in range(2):
                both = jnp.concatenate([ref[4 * ch + yl, far].astype(f32), ref[4 * ch + 2 + yl, far].astype(f32)], axis=0)
                w[pl.ds(row, OWN), ch * HD : (ch + 1) * HD] = both.astype(bf16)
            gap = pl.multiple_of(base + (1 - parity) * OWN, 16)
            w[pl.ds(gap, OWN), :] = jnp.zeros((OWN, 2 * HD), bf16)
        return 0

    lax.fori_loop(0, FAR, step, 0)


def project(hidden, w):
    return jnp.concatenate([dot(hidden[i : i + TOK // 2], w[:D, :], 1, 0) for i in (0, TOK // 2)], axis=0)


def prepare_body(hidden, queries, upstream, advantage, selected, q_gain, own, q_out, cot_out, kv_out, w):
    place(w, own, lax.axis_index("core"))
    kv_out[...] = project(hidden, w)
    weight = column(advantage[...] * selected[...].astype(f32))
    for h in range(GROUP):
        cols = slice(h * HD, (h + 1) * HD)
        query = queries[:, cols].astype(f32)
        q_scale = lax.rsqrt(jnp.mean(query * query, axis=-1, keepdims=True) + EPS)
        q_out[:, cols] = (query * q_scale * q_gain[...]).astype(bf16)
        cot_out[:, cols] = (weight * upstream[:, cols].astype(f32)).astype(bf16)


def backward_body(hidden, q_norms, cots, kv_part, segment, k_gain, other, keep, send, w, acc):
    core = lax.axis_index("core")
    place(w, other, 1 - core)
    kv = kv_part[...] + project(hidden, w)
    k_raw = kv[:, :HD]
    k_scale = lax.rsqrt(jnp.mean(k_raw * k_raw, axis=-1, keepdims=True) + EPS)
    k_hat = k_raw * k_scale
    k_norm = (k_hat * k_gain[...]).astype(bf16)
    values = kv[:, HD:].astype(bf16)
    seg = segment[...].astype(f32)
    seg_col = column(seg)
    s_col = lax.broadcasted_iota(jnp.int32, (TOK, HD), 0)
    t_row = lax.broadcasted_iota(jnp.int32, (TOK, HD), 1)
    allowed = jnp.concatenate(
        [(seg_col == seg[:, i * HD : (i + 1) * HD]) & (s_col <= t_row + i * HD) for i in range(2)], axis=1
    )
    scale = HD ** (-0.5)
    exponent = scale * 1.4426950408889634
    mask_low = allowed[:HD]
    mask_high = allowed[HD:, HD:]
    d_key_low = d_key_high = d_value_low = d_value_high = jnp.zeros((HD, HD), f32)
    for h in range(GROUP):
        cols = slice(h * HD, (h + 1) * HD)
        q_norm = q_norms[:, cols]
        cot = cots[:, cols]
        low, high = slice(0, HD), slice(HD, TOK)
        s_low = dot(k_norm[low], q_norm, 1, 1)
        s_high = dot(k_norm[high], q_norm[high], 1, 1)
        p_low = dot(values[low], cot, 1, 1)
        p_high = dot(values[high], cot[high], 1, 1)
        e_low = jnp.where(mask_low, jnp.exp2(s_low * exponent), 0.0)
        e_high = jnp.where(mask_high, jnp.exp2(s_high * exponent), 0.0)
        total = jnp.sum(e_low, axis=0, keepdims=True)
        total = jnp.concatenate([total[:, low], total[:, high] + jnp.sum(e_high, axis=0, keepdims=True)], axis=1)
        inverse = 1.0 / total
        e_low = e_low * inverse
        e_high = e_high * inverse[:, high]
        b_low = e_low.astype(bf16)
        b_high = e_high.astype(bf16)
        delta = jnp.sum(b_low.astype(f32) * p_low, axis=0, keepdims=True)
        delta = jnp.concatenate([delta[:, low], delta[:, high] + jnp.sum(b_high.astype(f32) * p_high, axis=0, keepdims=True)], axis=1)
        g_low = (e_low * (p_low - delta) * scale).astype(bf16)
        g_high = (e_high * (p_high - delta[:, high]) * scale).astype(bf16)
        d_key_low = d_key_low + dot(g_low, q_norm, 1, 0)
        d_key_high = d_key_high + dot(g_high, q_norm[high], 1, 0)
        d_value_low = d_value_low + dot(b_low, cot, 1, 0)
        d_value_high = d_value_high + dot(b_high, cot[high], 1, 0)
    d_key = jnp.concatenate([d_key_low, d_key_high], axis=0)
    d_value = jnp.concatenate([d_value_low, d_value_high], axis=0)
    gain = jnp.sum(d_key * k_hat, axis=0, keepdims=True)
    d_khat = d_key * k_gain[...]
    d_kraw = k_scale * (d_khat - k_hat * jnp.mean(d_khat * k_hat, axis=-1, keepdims=True))
    d_kv = jnp.concatenate([d_kraw, d_value], axis=1).astype(bf16)
    chunk = 1024
    for j in range(D // chunk):
        acc[j * chunk : (j + 1) * chunk, :] = dot(hidden[:, j * chunk : (j + 1) * chunk], d_kv, 0, 0)
    acc[D:SPAN, :] = jnp.zeros((SPAN - D, 2 * HD), f32)

    def put(far, _):
        for yl in range(2):
            base = first_row(far, yl)
            for parity, ref in ((core, keep), (1 - core, send)):
                for q in range(4):
                    row = pl.multiple_of(base + parity * OWN + (q % 2) * HALF, 8)
                    ref[2 * q + yl, far] = acc[pl.ds(row, HALF), (q // 2) * HD : (q // 2 + 1) * HD].astype(bf16)
        return 0

    lax.fori_loop(0, FAR, put, 0)
    high = gain.astype(bf16).astype(f32)
    line = lax.broadcasted_iota(jnp.int32, (HALF, HD), 0)
    rows = jnp.where(line == 0, high, jnp.where(line == 1, gain - high, 0.0)).astype(bf16)
    keep[1, FAR - 1] = rows
    send[1, FAR - 1] = rows


def gain_rows(pair):
    total = pair[0:1] + pair[1:2]
    high = total.astype(bf16).astype(f32)
    line = lax.broadcasted_iota(jnp.int32, (8, HD), 0)
    return jnp.where(line == 0, high, jnp.where(line == 1, total - high, 0.0))


def near_body(keep, received, blocks):
    tail = gain_rows(keep[1, FAR - 1, 0:8].astype(f32) + received[1, FAR - 1, 0:8].astype(f32))
    for i in range(NEAR):
        total = (keep[i].astype(f32) + received[i].astype(f32)).reshape(BODY, HD)
        if i % 2 == 1:
            total = jnp.concatenate([total[: BODY - HALF], jnp.zeros((HALF, HD), f32)], axis=0)
        blocks[i] = jnp.concatenate([total, tail], axis=0).astype(bf16)


def far_body(received, blocks):
    tail = gain_rows(sum(received[i, BODY:].astype(f32) for i in range(NEAR)))
    for far in range(0, FAR, 2):
        total = sum(received[i, far * HALF : (far + 2) * HALF].astype(f32) for i in range(NEAR))
        for i in range(2):
            blocks[far + i] = jnp.concatenate([total[i * HALF : (i + 1) * HALF], tail], axis=0).astype(bf16)


def last_body(received, blocks):
    total = sum(received[i].astype(f32) for i in range(FAR))
    whole = jnp.concatenate([total[:HALF], gain_rows(total[HALF:])], axis=0).astype(bf16)
    for i in range(16):
        blocks[i] = whole


def finish_body(spread, d_weight, d_gain):
    total = [sum(spread[8 * (i // 2) + 4 * (q // 2) + 2 * (i % 2) + q % 2].astype(f32) for i in range(4)) for q in range(4)]
    for q in range(4):
        row, col = (q % 2) * HALF, (q // 2) * HD
        d_weight[row : row + HALF, col : col + HD] = total[q][:HALF]
    d_gain[...] = total[0][HALF : HALF + 1] + total[0][HALF + 1 : HALF + 2]


def call(body, out, n_vector, scratch, limit, name):
    return pl.pallas_call(
        body,
        out_shape=out,
        in_specs=[vmem] * n_vector,
        out_specs=jax.tree.map(lambda _: vmem, out),
        scratch_shapes=scratch,
        compiler_params=pltpu.CompilerParams(vmem_limit_bytes=limit << 20),
        name=name,
    )


def shape(*dims, dtype=bf16):
    return jax.ShapeDtypeStruct(dims, dtype)


def near_groups():
    ids = np.arange(16 * 48).reshape(4, 4, 8, 3, 2)
    groups = []
    for core in range(2):
        for z in range(core, 12, 2):
            for x in range(core, 4, 2):
                for y in range(core, 8, 2):
                    members = [0] * NEAR
                    for i in range(NEAR):
                        mz, mx, my = (z + i // 4) % 12, (x + i // 2 % 2) % 4, (y + i % 2) % 8
                        members[4 * (mz % 2) + 2 * (mx % 2) + my % 2] = int(ids[mz % 4, mx, my, mz // 4, core])
                    groups.append(members)
    return groups


def exchange(x, axes, groups=None):
    return lax.all_to_all(x, axes, 0, 0, tiled=True, axis_index_groups=groups)


def swap(x):
    return lax.ppermute(x, "core", [(0, 1), (1, 0)])


def shards(hidden, queries, upstream, advantage, selected, segment, w_kv, k_gain, q_gain):
    mine = lax.dynamic_slice(w_kv, (lax.axis_index("xl") * HALF, lax.axis_index("zl") * HD), (HALF, HD))
    part = exchange(jnp.broadcast_to(mine[None], (FAR, HALF, HD)), ("yh", "zhi"))
    own = exchange(jnp.broadcast_to(part[None], (NEAR, FAR, HALF, HD)), AXES, near_groups())
    other = swap(own)
    w_scratch = pltpu.VMEM((SPAN, 2 * HD), bf16)
    q_norms, cots, kv_part = call(
        prepare_body, (shape(TOK, GROUP * HD), shape(TOK, GROUP * HD), shape(TOK, 2 * HD, dtype=f32)), 7, [w_scratch], 16, "prepare"
    )(hidden[0], queries[0], upstream[0], advantage, selected, q_gain[None], own)
    piece = shape(NEAR, FAR, HALF, HD)
    keep, send = call(backward_body, (piece, piece), 7, [w_scratch, pltpu.VMEM((SPAN, 2 * HD), f32)], 24, "backward")(
        hidden[0], q_norms, cots, kv_part, segment, k_gain[None], other
    )
    blocks = call(near_body, shape(NEAR, BODY + 8, HD), 2, [], 12, "near")(keep, swap(send))
    blocks = call(far_body, shape(FAR, HALF + 8, HD), 1, [], 12, "far")(exchange(blocks, AXES, near_groups()))
    blocks = call(last_body, shape(16, HALF + 8, HD), 1, [], 8, "last")(exchange(blocks, ("yh", "zhi")))
    spread = exchange(blocks, ("zh", "zl", "xh", "xl"))
    d_weight, d_gain = call(finish_body, (shape(OWN, 2 * HD, dtype=f32), shape(1, HD, dtype=f32)), 1, [], 4, "finish")(spread)
    return (d_weight, d_gain[0])


def solution(mesh):
    fine = Mesh(mesh.devices.reshape(2, 2, 2, 2, 4, 2, 3, 2), AXES)
    rows = P(AXES, None, None)
    flat = P(AXES, None)
    owners = P(("yh", "yl", "zhi", "core"), None)
    in_specs = (rows, rows, rows, flat, flat, flat, owners, P(), P())
    return jax.shard_map(shards, mesh=fine, in_specs=in_specs, out_specs=(owners, P()), check_vma=False)
```

```python
import jax
import jax.numpy as jnp
import numpy as np
from jax import lax
from jax.experimental import pallas as pl
from jax.experimental.pallas import tpu as pltpu
from jax.sharding import Mesh, PartitionSpec as P

EPS = 1e-06
HD = 128
GROUP = 8
TOK = 256
D = 5120
OWN = 112
HALF = OWN // 2
NEAR = 8
FAR = 12
BODY = FAR * HALF
SPAN = 48 * OWN
AXES = ("zh", "zl", "xh", "xl", "yh", "yl", "zhi", "core")

f32 = jnp.float32
bf16 = jnp.bfloat16
vmem = pl.BlockSpec(memory_space=pltpu.VMEM)


def dot(a, b, ca, cb):
    return lax.dot_general(a, b, (((ca,), (cb,)), ((), ())), preferred_element_type=f32)


def column(row):
    return jnp.transpose(jnp.broadcast_to(row, (HD, TOK)))


def first_row(far, yl):
    return ((far // 3) * 6 + yl * 3 + far % 3) * (2 * OWN)


def place(w, ref, parity):
    def step(far, _):
        for yl in range(2):
            base = first_row(far, yl)
            row = pl.multiple_of(base + parity * OWN, 16)
            for ch in range(2):
                both = jnp.concatenate([ref[4 * ch + yl, far].astype(f32), ref[4 * ch + 2 + yl, far].astype(f32)], axis=0)
                w[pl.ds(row, OWN), ch * HD : (ch + 1) * HD] = both.astype(bf16)
            gap = pl.multiple_of(base + (1 - parity) * OWN, 16)
            w[pl.ds(gap, OWN), :] = jnp.zeros((OWN, 2 * HD), bf16)
        return 0

    lax.fori_loop(0, FAR, step, 0)


def project(hidden, w):
    return jnp.concatenate([dot(hidden[i : i + TOK // 2], w[:D, :], 1, 0) for i in (0, TOK // 2)], axis=0)


def prepare_body(hidden, queries, upstream, advantage, selected, q_gain, own, q_out, cot_out, kv_out, w):
    place(w, own, lax.axis_index("core"))
    kv_out[...] = project(hidden, w)
    weight = column(advantage[...] * selected[...].astype(f32))
    for h in range(GROUP):
        cols = slice(h * HD, (h + 1) * HD)
        query = queries[:, cols].astype(f32)
        q_scale = lax.rsqrt(jnp.mean(query * query, axis=-1, keepdims=True) + EPS)
        q_out[:, cols] = (query * q_scale * q_gain[...]).astype(bf16)
        cot_out[:, cols] = (weight * upstream[:, cols].astype(f32)).astype(bf16)


def backward_body(hidden, q_norms, cots, kv_part, segment, k_gain, other, keep, send, w, acc):
    core = lax.axis_index("core")
    place(w, other, 1 - core)
    kv = kv_part[...] + project(hidden, w)
    k_raw = kv[:, :HD]
    k_scale = lax.rsqrt(jnp.mean(k_raw * k_raw, axis=-1, keepdims=True) + EPS)
    k_hat = k_raw * k_scale
    k_norm = (k_hat * k_gain[...]).astype(bf16)
    values = kv[:, HD:].astype(bf16)
    seg = segment[...].astype(f32)
    seg_col = column(seg)
    s_col = lax.broadcasted_iota(jnp.int32, (TOK, HD), 0)
    t_row = lax.broadcasted_iota(jnp.int32, (TOK, HD), 1)
    allowed = jnp.concatenate(
        [(seg_col == seg[:, i * HD : (i + 1) * HD]) & (s_col <= t_row + i * HD) for i in range(2)], axis=1
    )
    scale = HD ** (-0.5)
    exponent = scale * 1.4426950408889634
    mask_low = allowed[:HD]
    mask_high = allowed[HD:, HD:]
    d_key_low = d_key_high = d_value_low = d_value_high = jnp.zeros((HD, HD), f32)
    for h in range(GROUP):
        cols = slice(h * HD, (h + 1) * HD)
        q_norm = q_norms[:, cols]
        cot = cots[:, cols]
        low, high = slice(0, HD), slice(HD, TOK)
        s_low = dot(k_norm[low], q_norm, 1, 1)
        s_high = dot(k_norm[high], q_norm[high], 1, 1)
        p_low = dot(values[low], cot, 1, 1)
        p_high = dot(values[high], cot[high], 1, 1)
        e_low = jnp.where(mask_low, jnp.exp2(s_low * exponent), 0.0)
        e_high = jnp.where(mask_high, jnp.exp2(s_high * exponent), 0.0)
        total = jnp.sum(e_low, axis=0, keepdims=True)
        total = jnp.concatenate([total[:, low], total[:, high] + jnp.sum(e_high, axis=0, keepdims=True)], axis=1)
        inverse = 1.0 / total
        e_low = e_low * inverse
        e_high = e_high * inverse[:, high]
        b_low = e_low.astype(bf16)
        b_high = e_high.astype(bf16)
        delta = jnp.sum(b_low.astype(f32) * p_low, axis=0, keepdims=True)
        delta = jnp.concatenate([delta[:, low], delta[:, high] + jnp.sum(b_high.astype(f32) * p_high, axis=0, keepdims=True)], axis=1)
        g_low = (e_low * (p_low - delta) * scale).astype(bf16)
        g_high = (e_high * (p_high - delta[:, high]) * scale).astype(bf16)
        d_key_low = d_key_low + dot(g_low, q_norm, 1, 0)
        d_key_high = d_key_high + dot(g_high, q_norm[high], 1, 0)
        d_value_low = d_value_low + dot(b_low, cot, 1, 0)
        d_value_high = d_value_high + dot(b_high, cot[high], 1, 0)
    d_key = jnp.concatenate([d_key_low, d_key_high], axis=0)
    d_value = jnp.concatenate([d_value_low, d_value_high], axis=0)
    gain = jnp.sum(d_key * k_hat, axis=0, keepdims=True)
    d_khat = d_key * k_gain[...]
    d_kraw = k_scale * (d_khat - k_hat * jnp.mean(d_khat * k_hat, axis=-1, keepdims=True))
    d_kv = jnp.concatenate([d_kraw, d_value], axis=1).astype(bf16)
    chunk = 1024
    for j in range(D // chunk):
        acc[j * chunk : (j + 1) * chunk, :] = dot(hidden[:, j * chunk : (j + 1) * chunk], d_kv, 0, 0)
    acc[D:SPAN, :] = jnp.zeros((SPAN - D, 2 * HD), f32)

    def put(far, _):
        for yl in range(2):
            base = first_row(far, yl)
            for parity, ref in ((core, keep), (1 - core, send)):
                for q in range(4):
                    row = pl.multiple_of(base + parity * OWN + (q % 2) * HALF, 8)
                    ref[2 * q + yl, far] = acc[pl.ds(row, HALF), (q // 2) * HD : (q // 2 + 1) * HD].astype(bf16)
        return 0

    lax.fori_loop(0, FAR, put, 0)
    high = gain.astype(bf16).astype(f32)
    line = lax.broadcasted_iota(jnp.int32, (HALF, HD), 0)
    rows = jnp.where(line == 0, high, jnp.where(line == 1, gain - high, 0.0)).astype(bf16)
    keep[1, FAR - 1] = rows
    send[1, FAR - 1] = rows


def gain_rows(pair):
    total = pair[0:1] + pair[1:2]
    high = total.astype(bf16).astype(f32)
    line = lax.broadcasted_iota(jnp.int32, (8, HD), 0)
    return jnp.where(line == 0, high, jnp.where(line == 1, total - high, 0.0))


def near_body(keep, received, blocks):
    tail = gain_rows(keep[1, FAR - 1, 0:8].astype(f32) + received[1, FAR - 1, 0:8].astype(f32))
    for i in range(NEAR):
        total = (keep[i].astype(f32) + received[i].astype(f32)).reshape(BODY, HD)
        if i % 2 == 1:
            total = jnp.concatenate([total[: BODY - HALF], jnp.zeros((HALF, HD), f32)], axis=0)
        blocks[i] = jnp.concatenate([total, tail], axis=0).astype(bf16)


def far_body(received, blocks):
    tail = gain_rows(sum(received[i, BODY:].astype(f32) for i in range(NEAR)))
    for far in range(0, FAR, 2):
        total = sum(received[i, far * HALF : (far + 2) * HALF].astype(f32) for i in range(NEAR))
        for i in range(2):
            block = jnp.concatenate([total[i * HALF : (i + 1) * HALF], tail], axis=0).astype(bf16)
            blocks[far + i] = block
            blocks[FAR + far + i] = block


def last_body(received, blocks):
    total = sum(received[i].astype(f32) for i in range(2 * FAR))
    whole = jnp.concatenate([total[:HALF], gain_rows(total[HALF:])], axis=0).astype(bf16)
    for i in range(8):
        blocks[i] = whole


def finish_body(spread, d_weight, d_gain):
    total = [sum(spread[4 * i + q].astype(f32) for i in range(2)) for q in range(4)]
    for q in range(4):
        row, col = (q % 2) * HALF, (q // 2) * HD
        d_weight[row : row + HALF, col : col + HD] = total[q][:HALF]
    d_gain[...] = total[0][HALF : HALF + 1] + total[0][HALF + 1 : HALF + 2]


def call(body, out, n_vector, scratch, limit, name):
    return pl.pallas_call(
        body,
        out_shape=out,
        in_specs=[vmem] * n_vector,
        out_specs=jax.tree.map(lambda _: vmem, out),
        scratch_shapes=scratch,
        compiler_params=pltpu.CompilerParams(vmem_limit_bytes=limit << 20),
        name=name,
    )


def shape(*dims, dtype=bf16):
    return jax.ShapeDtypeStruct(dims, dtype)


def near_groups():
    ids = np.arange(16 * 48).reshape(4, 4, 8, 3, 2)
    groups = []
    for core in range(2):
        for z in range(core, 12, 2):
            for x in range(core, 4, 2):
                for y in range(core, 8, 2):
                    members = [0] * NEAR
                    for i in range(NEAR):
                        mz, mx, my = (z + i // 4) % 12, (x + i // 2 % 2) % 4, (y + i % 2) % 8
                        members[4 * (mz % 2) + 2 * (mx % 2) + my % 2] = int(ids[mz % 4, mx, my, mz // 4, core])
                    groups.append(members)
    return groups


def exchange(x, axes, groups=None):
    return lax.all_to_all(x, axes, 0, 0, tiled=True, axis_index_groups=groups)


def swap(x):
    return lax.ppermute(x, "core", [(0, 1), (1, 0)])


def shards(hidden, queries, upstream, advantage, selected, segment, w_kv, k_gain, q_gain):
    mine = lax.dynamic_slice(w_kv, (lax.axis_index("xl") * HALF, lax.axis_index("zl") * HD), (HALF, HD))
    part = exchange(jnp.broadcast_to(mine[None], (FAR, HALF, HD)), ("yh", "zhi"))
    own = exchange(jnp.broadcast_to(part[None], (NEAR, FAR, HALF, HD)), AXES, near_groups())
    other = swap(own)
    w_scratch = pltpu.VMEM((SPAN, 2 * HD), bf16)
    q_norms, cots, kv_part = call(
        prepare_body, (shape(TOK, GROUP * HD), shape(TOK, GROUP * HD), shape(TOK, 2 * HD, dtype=f32)), 7, [w_scratch], 16, "prepare"
    )(hidden[0], queries[0], upstream[0], advantage, selected, q_gain[None], own)
    piece = shape(NEAR, FAR, HALF, HD)
    keep, send = call(backward_body, (piece, piece), 7, [w_scratch, pltpu.VMEM((SPAN, 2 * HD), f32)], 24, "backward")(
        hidden[0], q_norms, cots, kv_part, segment, k_gain[None], other
    )
    blocks = call(near_body, shape(NEAR, BODY + 8, HD), 2, [], 12, "near")(keep, swap(send))
    blocks = call(far_body, shape(2 * FAR, HALF + 8, HD), 1, [], 12, "far")(exchange(blocks, AXES, near_groups()))
    blocks = call(last_body, shape(8, HALF + 8, HD), 1, [], 8, "last")(exchange(blocks, ("xh", "yh", "zhi")))
    spread = exchange(blocks, ("zh", "zl", "xl"))
    d_weight, d_gain = call(finish_body, (shape(OWN, 2 * HD, dtype=f32), shape(1, HD, dtype=f32)), 1, [], 4, "finish")(spread)
    return (d_weight, d_gain[0])


def solution(mesh):
    fine = Mesh(mesh.devices.reshape(2, 2, 2, 2, 4, 2, 3, 2), AXES)
    rows = P(AXES, None, None)
    flat = P(AXES, None)
    owners = P(("yh", "yl", "zhi", "core"), None)
    in_specs = (rows, rows, rows, flat, flat, flat, owners, P(), P())
    return jax.shard_map(shards, mesh=fine, in_specs=in_specs, out_specs=(owners, P()), check_vma=False)
```
